32 devices in a mesh: dp: 2 (over core), expert: 16 (over z, y, x), tensor: 1.
Axes of the slice: x: 2, y: 2, z: 4, core: 2. Of those that a mesh axis runs over, the one named last changes fastest.
Arguments:
- tokens: bfloat16 [2048, 3584], P('expert'), may hold values from -6 to 6
- shared_gate_w: bfloat16 [3584, 10240], P(None, ('dp', 'tensor')), may hold values from -0.09375 to 0.09375
- shared_up_w: bfloat16 [3584, 10240], P(None, ('dp', 'tensor')), may hold values from -0.09375 to 0.09375
- shared_down_w: bfloat16 [10240, 3584], P(('dp', 'tensor')), may hold values from -0.0625 to 0.0625
- routed_gate_w: bfloat16 [16, 3584, 2560], P('expert', 'dp', 'tensor'), may hold values from -0.09375 to 0.09375
- routed_up_w: bfloat16 [16, 3584, 2560], P('expert', 'dp', 'tensor'), may hold values from -0.09375 to 0.09375
- routed_down_w: bfloat16 [16, 2560, 3584], P('expert', 'tensor', 'dp'), may hold values from -0.125 to 0.125
- expert_ids: int32 [2048, 8], P('expert'), may hold values from 0 to 15, all different within a row; in each aligned block of 128 rows (0 to 127, 128 to 255, ...) at most 96 rows name the same one
- gate_weights: bfloat16 [2048, 8], P('expert'), may hold values from 0.049804688 to 1
Outputs:
- mixed_out: bfloat16 [2048, 3584], P('expert', ('dp', 'tensor'))
- balance: float32 [16], P('expert')
The draws below stay inside these ranges and needn't reach their ends.
Inputs may be any that keep to these rules, and one draw needn't show every extreme that they name: `expert_ids`: each row names 8 different experts; within the 128 rows of one index of the expert axis no expert is named by more than 96 rows, a bound that some block reaches.
All inputs are finite; a program needn't handle non-finite values.
Results may differ from the reference program's by a relative error of at most 0.0054.
Values may be sent and summed in bfloat16 or wider, within the bound.
A program may use at most 256 MiB of HBM per device.

```python
import math
import jax
import jax.numpy as jnp
import numpy as np
from jax import lax

D = 3584
FS = 10240
FE = 2560
TOPK = 8
TOK_DEV = 128
EXPERTS = 16
CAP = 96
TOKENS = 2048
N_EXPERT = 16
N_TENSOR = 1


def steps_of(rng, shape, cuts, smallest, top_value):
    def one(axis_at, shards_of):
        draws = jax.random.uniform(jax.random.fold_in(jax.random.fold_in(rng, 6), axis_at), (shards_of,), jnp.float32, smallest / len(cuts), top_value / len(cuts))
        return jnp.repeat(jnp.exp(draws), shape[axis_at] // shards_of).reshape((-1,) + (1,) * (len(shape) - axis_at - 1))

    loudness = one(*cuts[0])
    for cut in cuts[1:]:
        loudness = loudness * one(*cut)
    return loudness


def deal_out(own_key, own, number, rows, amount, top, most, skew):
    order = jax.random.permutation(own_key, amount)
    packed, common = portions_of(amount, rows * top, most, skew, True), portions_of(amount, rows * top, most, skew, False)
    places = jnp.arange(amount)

    def named(lengths, offset_by):
        used = int((lengths > 0).sum())
        fixed = max(1, used // 4)
        moved = fixed + (places - fixed + offset_by * (used - fixed)) % max(1, amount - fixed)
        return jnp.zeros((amount,), jnp.int32).at[order[jnp.where(places < fixed, places, moved)]].set(jnp.asarray(lengths, jnp.int32))

    lengths = jnp.where(number % 4 == 0, named(packed, number // 4), named(common, number - number // 4 - 1))
    mixed = jax.random.permutation(jax.random.fold_in(own, 3), amount)
    donor, sink = mixed[0:amount // 2 * 2:2], mixed[1:amount // 2 * 2:2]
    room = jnp.minimum(lengths[donor] - 1, most - lengths[sink]) // 2
    room = jnp.where((donor == order[0]) | (sink == order[0]) | (lengths[sink] == 0), 0, jnp.maximum(room, 0))
    moved = jax.random.randint(jax.random.fold_in(own, 4), (amount // 2,), 0, 1 << 20) % (room + 1)
    lengths = lengths.at[donor].add(-moved).at[sink].add(moved)
    items = jnp.searchsorted(jnp.cumsum(lengths), jnp.arange(rows * top), side="right").astype(jnp.int32)
    listing = items.reshape(top, rows).T
    listing = listing[jax.random.permutation(jax.random.fold_in(own, 1), rows)]
    offset_by = jax.random.randint(jax.random.fold_in(own, 2), (rows, 1), 0, top)
    return jnp.take_along_axis(listing, (jnp.arange(top)[None, :] + offset_by) % top, axis=1)


def portions_of(amount, total, bound, lean, full):
    portions = [(1 << 20) // math.isqrt(rank ** lean) + 1 for rank in range(1, amount + 1)]
    largest = bound if full else min(bound, max(-(-total // amount), total * portions[0] // sum(portions)))
    least = 1 if total - largest >= amount - 1 else 0
    given, spare = [largest] + [least] * (amount - 1), total - largest - least * (amount - 1)
    while spare > 0:
        candidates = [i for i in range(1, amount) if given[i] < largest] or [i for i in range(1, amount) if given[i] < bound]
        pool, budget = sum([portions[i] for i in candidates]), spare
        for i in candidates:
            extra = min(bound - given[i], max(1, budget * portions[i] // pool), spare)
            given[i] = given[i] + extra
            spare = spare - extra
    return np.array(given)


def normal_values(stream_key, shape, deviation, limit, shards=(), kind=jnp.bfloat16):
    gain = steps_of(stream_key, shape, shards, -0.22, 0.18) if shards else 1.0
    entries = jax.random.normal(stream_key, shape, jnp.float32) * deviation * gain
    return jnp.minimum(jnp.maximum(entries, -limit), limit).astype(kind)


def setup_inputs(seed: int = 0) -> dict:
    key_list = jax.random.split(jax.random.key(seed), 10)
    tokens = normal_values(key_list[0], (TOKENS, D), 1.0, 6.0, ((0, 16),))
    shared_gate_w = normal_values(key_list[1], (D, FS), D ** -0.5, 0.09375, ((1, 2),))
    shared_up_w = normal_values(key_list[2], (D, FS), D ** -0.5, 0.09375, ((1, 2),))
    shared_down_w = normal_values(key_list[3], (FS, D), FS ** -0.5, 0.0625, ((0, 2),))
    routed_gate_w = normal_values(key_list[4], (EXPERTS, D, FE), D ** -0.5, 0.09375, ((0, 16), (1, 2)))
    routed_up_w = normal_values(key_list[5], (EXPERTS, D, FE), D ** -0.5, 0.09375, ((0, 16), (1, 2)))
    routed_down_w = normal_values(key_list[6], (EXPERTS, FE, D), FE ** -0.5, 0.125, ((0, 16), (2, 2)))
    expert_ids_keys = jax.random.split(jax.random.fold_in(key_list[7], 1), TOKENS // TOK_DEV)
    expert_ids_turns = jax.random.permutation(jax.random.fold_in(key_list[7], 3), TOKENS // TOK_DEV)
    expert_ids = jax.vmap(lambda own, number: deal_out(jax.random.fold_in(key_list[7], 2), own, number, TOK_DEV, EXPERTS, TOPK, CAP, 1))(expert_ids_keys, expert_ids_turns).reshape((TOKENS, TOPK))
    gate_weights = jnp.clip(jnp.exp(math.log(1.0) - 2.9996462 * jax.random.uniform(key_list[8], (TOKENS, TOPK), jnp.float32) ** steps_of(key_list[8], (TOKENS, TOPK), ((0, 16),), -0.2, 0.2)), 0.049804688, 1.0).astype(jnp.bfloat16)
    return dict(tokens=tokens, shared_gate_w=shared_gate_w, shared_up_w=shared_up_w, shared_down_w=shared_down_w, routed_gate_w=routed_gate_w, routed_up_w=routed_up_w, routed_down_w=routed_down_w, expert_ids=expert_ids, gate_weights=gate_weights)


def reference(tokens, shared_gate_w, shared_up_w, shared_down_w, routed_gate_w, routed_up_w, routed_down_w, expert_ids, gate_weights):
    shared_gate = jnp.dot(tokens, shared_gate_w, preferred_element_type=jnp.float32)
    shared_up = jnp.dot(tokens, shared_up_w, preferred_element_type=jnp.float32)
    shared_hidden = (jax.nn.silu(shared_gate) * shared_up).astype(jnp.bfloat16)
    shared_out = jnp.dot(shared_hidden, shared_down_w, preferred_element_type=jnp.float32)
    row_limit = CAP * N_EXPERT
    block_units = FE // N_TENSOR
    token_iota = jnp.arange(TOKENS, dtype=jnp.int32)
    slot_iota = jnp.arange(row_limit, dtype=jnp.int32)
    gate_float = gate_weights.astype(jnp.float32)

    def add_expert(total, inputs):
        gate_mat, up_mat, down_mat, expert = inputs
        named = expert_ids == expert
        has_token = jnp.any(named, axis=1)
        token_gate = jnp.sum(jnp.where(named, gate_float, jnp.float32(0.0)), axis=1)
        running = jnp.cumsum(has_token.astype(jnp.int32))
        target = jnp.where(has_token, running - 1, row_limit).astype(jnp.int32)
        source = jnp.zeros((row_limit,), jnp.int32).at[target].set(token_iota, mode="drop")
        valid = (slot_iota < running[-1]).astype(jnp.float32)
        rows = tokens[source]
        gate_val = jnp.dot(rows, gate_mat, preferred_element_type=jnp.float32)
        up_val = jnp.dot(rows, up_mat, preferred_element_type=jnp.float32)
        hidden = (jax.nn.silu(gate_val) * up_val).astype(jnp.bfloat16)
        blocks = jnp.einsum("rnf,nfd->rnd", hidden.reshape(row_limit, N_TENSOR, block_units).astype(jnp.float32), down_mat.reshape(N_TENSOR, block_units, D).astype(jnp.float32), precision=lax.Precision.HIGHEST)
        scale = token_gate[source] * valid
        rounded = (blocks * scale[:, None, None]).astype(jnp.bfloat16)
        rounded = lax.optimization_barrier(rounded)
        parts = jnp.sum(rounded.astype(jnp.float32), axis=1)
        stats = (jnp.sum(has_token.astype(jnp.float32)), jnp.sum(token_gate))
        return total.at[source].add(parts), stats

    routed, stats = lax.scan(add_expert, jnp.zeros((TOKENS, D), jnp.float32), (routed_gate_w, routed_up_w, routed_down_w, jnp.arange(EXPERTS, dtype=jnp.int32)))
    counts, totals = stats
    balance = EXPERTS * (counts / (TOKENS * TOPK)) * (totals / TOKENS)
    mixed_out = (shared_out + routed).astype(jnp.bfloat16)
    return mixed_out, balance
```

```python
import jax
import jax.numpy as jnp
from jax import lax
from jax.sharding import PartitionSpec as P


BF16 = jnp.bfloat16
F32 = jnp.float32


def dot(a, b):
    return jnp.dot(a, b, preferred_element_type=F32)


def shards(
    tokens,
    shared_gate_w,
    shared_up_w,
    shared_down_w,
    routed_gate_w,
    routed_up_w,
    routed_down_w,
    expert_ids,
    gate_weights,
):
    rows, top_count = expert_ids.shape
    groups = lax.axis_size("expert")
    planes = groups // 4
    experts_all = routed_gate_w.shape[0] * groups
    capacity = min(rows, max(2, 3 * rows * top_count // (2 * experts_all)))
    half = routed_gate_w.shape[1]
    units = routed_gate_w.shape[2] // 2
    core = lax.axis_index("dp")
    me = lax.axis_index("expert")
    first = core == 0
    both = ("dp", "expert")

    def send(value, targets):
        pairs = [
            (d * groups + e, d * groups + targets[d](e)) for d in range(2) for e in range(groups)
        ]
        return lax.ppermute(value, both, pairs)

    def swap_cores(value):
        return lax.ppermute(value, "dp", [(0, 1), (1, 0)])

    def shift(value, planes_up):
        to = lambda e: (e + 4 * planes_up) % groups
        return send(value, (to, to))

    flip_x = lambda e: e ^ 1
    flip_y = lambda e: e ^ 2

    tokens_half = lax.dynamic_slice_in_dim(tokens, core * half, half, 1)

    chosen = expert_ids[:, :, None] == jnp.arange(experts_all, dtype=jnp.int32)[None, None, :]
    gate_table = jnp.sum(
        jnp.where(chosen, gate_weights.astype(F32)[:, :, None], 0.0), axis=1
    ).astype(BF16)
    all_table = lax.all_gather(gate_table, "expert", axis=0, tiled=True)
    own_table = jnp.sum(
        jnp.where(jnp.arange(experts_all)[None, :] == me, all_table.astype(F32), 0.0), axis=1
    ).reshape(groups, rows)
    counts = jnp.sum((own_table > 0).astype(F32))[None]
    totals = jnp.sum(own_table)[None]
    token_total = rows * groups
    balance = experts_all * (counts / (token_total * top_count)) * (totals / token_total)

    place = jnp.arange(groups, dtype=jnp.int32)
    source = ((me // 4 + place // 4) % planes) * 4 + ((me % 4) ^ (place % 4))
    reorder = (source[:, None] == place[None, :]).astype(F32)
    table = jnp.dot(reorder, own_table, precision=lax.Precision.HIGHEST)
    present = table > 0
    upto = (jnp.arange(rows)[:, None] <= jnp.arange(rows)[None, :]).astype(BF16)
    slot = dot(present.astype(BF16), upto).astype(jnp.int32) - 1
    pick = (
        (slot[:, None, :] == jnp.arange(capacity, dtype=jnp.int32)[None, :, None])
        & present[:, None, :]
    )
    slot_gate = jnp.sum(jnp.where(pick, table[:, None, :], 0.0), axis=2)
    pick = pick.astype(BF16)

    gate_w, up_w, down_w = routed_gate_w[0], routed_up_w[0], routed_down_w[0]
    gate_own = lax.dynamic_slice_in_dim(gate_w, core * units, units, 1)
    up_own = lax.dynamic_slice_in_dim(up_w, core * units, units, 1)
    gate_other = swap_cores(lax.dynamic_slice_in_dim(gate_w, (1 - core) * units, units, 1))
    up_other = swap_cores(lax.dynamic_slice_in_dim(up_w, (1 - core) * units, units, 1))

    def gather_plane(s):
        block = tokens_half if s == 0 else shift(tokens_half, planes - s)
        near = send(block, (flip_x, flip_y))
        pair = jnp.stack([block, near])
        far = send(pair, (flip_y, flip_x))
        return jnp.stack(
            [block, jnp.where(first, near, far[0]), jnp.where(first, far[0], near), far[1]]
        )

    def expert_plane(s, blocks):
        picked = pick[4 * s : 4 * s + 4]
        mine = jnp.einsum("gct,gtd->gcd", picked, blocks, preferred_element_type=F32)
        mine = mine.astype(BF16).reshape(4 * capacity, half)
        other = swap_cores(mine)
        gate = dot(mine, gate_own) + dot(other, gate_other)
        up = dot(mine, up_own) + dot(other, up_other)
        hidden = (jax.nn.silu(gate) * up).astype(BF16)
        hidden_other = swap_cores(hidden)
        hidden_all = jnp.concatenate(
            [jnp.where(first, hidden, hidden_other), jnp.where(first, hidden_other, hidden)], axis=1
        )
        out = dot(hidden_all, down_w)
        scaled = (out * slot_gate[4 * s : 4 * s + 4].reshape(-1)[:, None]).astype(BF16)
        return jnp.einsum(
            "gct,gcd->gtd", picked, scaled.reshape(4, capacity, half), preferred_element_type=F32
        ).astype(BF16)

    def return_plane(s, dense):
        away = jnp.stack([jnp.where(first, dense[2], dense[1]), dense[3]])
        got = send(away, (flip_y, flip_x)).astype(F32)
        near = (jnp.where(first, dense[1], dense[2]).astype(F32) + got[1]).astype(BF16)
        got_near = send(near, (flip_x, flip_y)).astype(F32)
        total = dense[0].astype(F32) + got[0] + got_near
        if s == 0:
            return total
        return shift(total.astype(BF16), s).astype(F32)

    gathered = [gather_plane(s) for s in range(planes)]

    shared_gate = dot(tokens, shared_gate_w)
    shared_up = dot(tokens, shared_up_w)
    shared_hidden = (jax.nn.silu(shared_gate) * shared_up).astype(BF16)
    shared_part = dot(shared_hidden, shared_down_w)
    result = lax.dynamic_slice_in_dim(shared_part, core * half, half, 1) + swap_cores(
        lax.dynamic_slice_in_dim(shared_part, (1 - core) * half, half, 1)
    )

    for s in range(planes):
        result = result + return_plane(s, expert_plane(s, gathered[s]))
    if lax.axis_size("tensor") > 1:
        result = lax.psum_scatter(result, "tensor", scatter_dimension=1, tiled=True)
    return (result.astype(BF16), balance)


def solution(mesh):
    in_specs = (
        P("expert", None),
        P(None, ("dp", "tensor")),
        P(None, ("dp", "tensor")),
        P(("dp", "tensor"), None),
        P("expert", "dp", "tensor"),
        P("expert", "dp", "tensor"),
        P("expert", "tensor", "dp"),
        P("expert", None),
        P("expert", None),
    )
    out_specs = (P("expert", ("dp", "tensor")), P("expert"))
    return jax.shard_map(shards, mesh=mesh, in_specs=in_specs, out_specs=out_specs, check_vma=False)
```

```python
import jax
import jax.numpy as jnp
from jax import lax
from jax.sharding import PartitionSpec as P


BF16 = jnp.bfloat16
F32 = jnp.float32


def dot(a, b):
    return jnp.dot(a, b, preferred_element_type=F32)


def shards(
    tokens,
    shared_gate_w,
    shared_up_w,
    shared_down_w,
    routed_gate_w,
    routed_up_w,
    routed_down_w,
    expert_ids,
    gate_weights,
):
    rows, top_count = expert_ids.shape
    groups = lax.axis_size("expert")
    planes = groups // 4
    experts_all = routed_gate_w.shape[0] * groups
    capacity = min(rows, max(2, 3 * rows * top_count // (2 * experts_all)))
    half = routed_gate_w.shape[1]
    units = routed_gate_w.shape[2] // 2
    core = lax.axis_index("dp")
    me = lax.axis_index("expert")
    first = core == 0
    both = ("dp", "expert")

    def send(value, targets):
        pairs = [
            (d * groups + e, d * groups + targets[d](e)) for d in range(2) for e in range(groups)
        ]
        return lax.ppermute(value, both, pairs)

    def swap_cores(value):
        return lax.ppermute(value, "dp", [(0, 1), (1, 0)])

    def shift(value, planes_up):
        to = lambda e: (e + 4 * planes_up) % groups
        return send(value, (to, to))

    flip_x = lambda e: e ^ 1
    flip_y = lambda e: e ^ 2

    chosen = expert_ids.T[None, :, :] == jnp.arange(experts_all, dtype=jnp.int32)[:, None, None]
    gate_table = jnp.sum(jnp.where(chosen, gate_weights.T.astype(F32)[None, :, :], 0.0), axis=1)
    gate_table = jnp.pad(gate_table.astype(BF16), ((0, -experts_all % 16), (0, 0)))
    bands = gate_table.shape[0] // 16
    table_rows = jnp.concatenate([gate_table[16 * j : 16 * j + 16] for j in range(bands)], axis=1)
    table_rows = jnp.pad(table_rows, ((0, 0), (0, half - bands * rows)))
    own_block = jnp.concatenate(
        [lax.dynamic_slice_in_dim(tokens, core * half, half, 1), table_rows], axis=0
    )

    near, side, far = {}, {}, {}
    block = {0: own_block}
    near[0] = send(own_block, (flip_x, flip_y))
    side[0] = send(own_block, (flip_y, flip_x))
    order = [s for s in range(1, planes)]
    order.sort(key=lambda s: min(s, planes - s))
    for s in order:
        block[s] = shift(own_block, planes - s)

    gate_w, up_w, down_w = routed_gate_w[0], routed_up_w[0], routed_down_w[0]

    def whole_width(weight):
        kept = lax.dynamic_slice_in_dim(weight, core * units, units, 1)
        got = swap_cores(lax.dynamic_slice_in_dim(weight, (1 - core) * units, units, 1))
        return kept, got

    gate_kept, gate_got = whole_width(gate_w)
    up_kept, up_got = whole_width(up_w)

    tokens_a, near[0] = lax.optimization_barrier((tokens, near[0]))
    far[0] = send(near[0], (flip_y, flip_x))
    shared_gate = dot(tokens_a, shared_gate_w)
    early = order[: len(order) // 2 + 1]
    late = order[len(order) // 2 + 1 :]
    tokens_b, shared_gate, got = lax.optimization_barrier(
        (tokens_a, shared_gate, [block[s] for s in early])
    )
    for s, value in zip(early, got):
        near[s] = send(value, (flip_x, flip_y))
        side[s] = send(value, (flip_y, flip_x))
        block[s] = value
    shared_up = dot(tokens_b, shared_up_w)
    shared_hidden = (jax.nn.silu(shared_gate) * shared_up).astype(BF16)
    shared_hidden, got, got_late = lax.optimization_barrier(
        (shared_hidden, [near[s] for s in early], [block[s] for s in late])
    )
    for s, value in zip(early, got):
        far[s] = send(value, (flip_y, flip_x))
        near[s] = value
    for s, value in zip(late, got_late):
        near[s] = send(value, (flip_x, flip_y))
        side[s] = send(value, (flip_y, flip_x))
        block[s] = value
    shared_part = dot(shared_hidden, shared_down_w)
    shared_part, got_late = lax.optimization_barrier((shared_part, [near[s] for s in late]))
    for s, value in zip(late, got_late):
        far[s] = send(value, (flip_y, flip_x))
        near[s] = value
    result = lax.dynamic_slice_in_dim(shared_part, core * half, half, 1) + swap_cores(
        lax.dynamic_slice_in_dim(shared_part, (1 - core) * half, half, 1)
    )

    upto = (jnp.arange(rows)[:, None] <= jnp.arange(rows)[None, :]).astype(BF16)
    picks, slot_gates, tables, mine, other = {}, {}, {}, {}, {}

    def dispatch(s):
        arrived = [block[s], near[s], side[s], far[s]]
        at = (rows + me % 16, (me // 16) * rows)
        table = jnp.concatenate(
            [lax.dynamic_slice(value, at, (1, rows)) for value in arrived], axis=0
        ).astype(F32)
        present = table > 0
        slot = dot(present.astype(BF16), upto).astype(jnp.int32) - 1
        lines = jnp.arange(4 * capacity, dtype=jnp.int32)[:, None]
        swapped = jnp.where(first, 1, 2)
        start = jnp.array([0, 1, 2, 3]) * capacity
        start = start.at[1].set(swapped * capacity).at[2].set((3 - swapped) * capacity)
        wanted = jnp.where(present, slot + start[:, None], -1)
        pick = lines == wanted.reshape(1, 4 * rows)
        slot_gates[s] = jnp.sum(jnp.where(pick, table.reshape(1, 4 * rows), 0.0), axis=1)
        wanted = jnp.pad(wanted, ((0, 0), (0, 16)), constant_values=-1)
        fetch = (lines == wanted.reshape(1, 4 * (rows + 16))).astype(BF16)
        picks[s] = pick.astype(BF16)
        tables[s] = table
        mine[s] = dot(fetch, jnp.concatenate(arrived, axis=0)).astype(BF16)
        other[s] = swap_cores(mine[s])

    def hidden_of(s):
        gate = dot(mine[s], gate_kept) + dot(other[s], gate_got)
        up = dot(mine[s], up_kept) + dot(other[s], up_got)
        return (jax.nn.silu(gate) * up).astype(BF16)

    def dense_of(s, hidden, hidden_other):
        hidden_all = jnp.concatenate(
            [jnp.where(first, hidden, hidden_other), jnp.where(first, hidden_other, hidden)], axis=1
        )
        out = dot(hidden_all, down_w)
        scaled = (out * slot_gates[s][:, None]).astype(BF16)
        scaled = lax.optimization_barrier(scaled)
        return [
            lax.dot_general(
                part, scaled, (((0,), (0,)), ((), ())), preferred_element_type=F32
            ).astype(BF16)
            for part in (picks[s][:, : 2 * rows], picks[s][:, 2 * rows :])
        ]

    visits = order + [0]
    dispatch(visits[0])
    hidden = {}
    waiting = []

    def away_stage(dense):
        return dense[0], send(dense[1], (flip_y, flip_x))

    def near_stage(dense, got):
        total = dense.astype(F32) + got.astype(F32)
        return total[:rows], send(total[rows:].astype(BF16), (flip_x, flip_y))

    def plane_stage(s, kept, got):
        total = kept + got.astype(F32)
        return total if s == 0 else shift(total.astype(BF16), s)

    def advance(token):
        nonlocal waiting
        token, states = lax.optimization_barrier((token, [state for _, _, state in waiting]))
        moved = []
        for (s, stage, _), state in zip(waiting, states):
            if stage == 0:
                moved.append((s, 1, near_stage(*state)))
            elif stage == 1:
                moved.append((s, 2, plane_stage(s, *state)))
            else:
                moved.append((s, 2, state))
        waiting = moved
        return token

    for i, s in enumerate(visits + [None]):
        if s is not None:
            if i > 0:
                mine[s], other[s], _ = lax.optimization_barrier(
                    (mine[s], other[s], hidden[visits[i - 1]])
                )
            if i + 1 < len(visits):
                dispatch(visits[i + 1])
                mine[s], other[s], mine[visits[i + 1]] = lax.optimization_barrier(
                    (mine[s], other[s], mine[visits[i + 1]])
                )
            hidden[s] = hidden_of(s)
        if i > 0:
            back = visits[i - 1]
            hidden_other = swap_cores(hidden[back])
            kept = hidden[back]
            if s is not None:
                kept, hidden_other, hidden[s] = lax.optimization_barrier(
                    (kept, hidden_other, hidden[s])
                )
                kept = advance(kept)
            waiting.append((back, 0, away_stage(dense_of(back, kept, hidden_other))))
    for s, stage, state in reversed(waiting):
        if stage == 0:
            state = near_stage(*state)
        if stage < 2:
            state = plane_stage(s, *state)
        result = result + state.astype(F32)
    every = jnp.concatenate([tables[s] for s in visits], axis=0)
    token_total = rows * groups
    counts = jnp.sum((every > 0).astype(F32))[None]
    totals = jnp.sum(every)[None]
    balance = experts_all * (counts / (token_total * top_count)) * (totals / token_total)
    if lax.axis_size("tensor") > 1:
        result = lax.psum_scatter(result, "tensor", scatter_dimension=1, tiled=True)
    return (result.astype(BF16), balance)


def solution(mesh):
    in_specs = (
        P("expert", None),
        P(None, ("dp", "tensor")),
        P(None, ("dp", "tensor")),
        P(("dp", "tensor"), None),
        P("expert", "dp", "tensor"),
        P("expert", "dp", "tensor"),
        P("expert", "tensor", "dp"),
        P("expert", None),
        P("expert", None),
    )
    out_specs = (P("expert", ("dp", "tensor")), P("expert"))
    return jax.shard_map(shards, mesh=mesh, in_specs=in_specs, out_specs=out_specs, check_vma=False)
```
